256 devices in a mesh: band: 32 (over x_hi, z, core), fft: 8 (over x_lo, y).
Axes of the slice: x: 4 (x_hi: 2, x_lo: 2; x = x_hi * 2 + x_lo), y: 4, z: 8, core: 2. Of those that a mesh axis runs over, the one named last changes fastest.
Arguments:
- orbitals: float32 [64, 64, 4096], P('band', 'fft'), may hold values from -5 to 5
Outputs:
- exchange: float32 [64, 64, 4096], P('band', 'fft')
The draws below stay inside these ranges and needn't reach their ends.
All inputs are finite; a program needn't handle non-finite values.
Results may differ from the reference program's by a relative error of at most 0.00018.
Values sent between devices are 32-bit elements; how exact they have to be, the bound alone decides.
No kernel may reach another device: no remote copies, remote signals or barrier semaphores. Data moves between devices by JAX's collectives and lax.ppermute only.
A program may use at most 64 MiB of HBM per device.

```python
import math
import jax
import jax.numpy as jnp
from jax import lax

GRID = 64
ORB_DEV = 2
ROUNDS = 2
NORB = 64


def draw_orbitals(key, part):
    rough_key = jax.random.fold_in(key, 0)
    shape = (NORB, GRID, GRID * GRID)
    rough = jax.random.normal(rough_key, shape, jnp.float32)
    return jnp.clip(rough, -5.0, 5.0)


def setup_inputs(seed: int = 0) -> dict:
    arg_keys = jax.random.split(jax.random.key(seed), 2)
    return {
        "orbitals": draw_orbitals(jax.random.fold_in(arg_keys[1], 71), 0),
    }


EXX_FRACTION = 0.25
SCREEN = 0.05


def kernel_table(length):
    indices = jnp.arange(length, dtype=jnp.int32)
    signed = jnp.where(indices < length // 2, indices, indices - length).astype(jnp.float32)
    wavenum = signed * (2.0 * math.pi / length)
    squares = wavenum[:, None, None] ** 2 + wavenum[None, :, None] ** 2 + wavenum[None, None, :] ** 2
    guarded = jnp.where(squares > 0, squares, 1.0)
    return jnp.where(squares > 0, (1.0 - jnp.exp(-guarded / (4.0 * SCREEN * SCREEN))) / guarded, 0.0)


def reference(orbitals):
    fields = orbitals.reshape(NORB, GRID, GRID, GRID)
    sources = fields[: ROUNDS * ORB_DEV]
    kernel = kernel_table(GRID)

    def apply_one(orbital):
        density = orbital[None] * sources
        spectrum = jnp.fft.fftn(density, axes=(1, 2, 3))
        potential = jnp.real(jnp.fft.ifftn(spectrum * kernel, axes=(1, 2, 3)))
        return -EXX_FRACTION * jnp.sum(sources * potential, axis=0)

    result = lax.map(apply_one, fields)
    return result.reshape(NORB, GRID, GRID * GRID)
```

```python
import math

import jax
import jax.numpy as jnp
from jax import lax
from jax.sharding import PartitionSpec as P

GRID = 64
EXX_FRACTION = 0.25
SCREEN = 0.05
CHIPS = 16


def angle_tables(length):
    indices = jnp.arange(length, dtype=jnp.int32)
    residue = indices[:, None] * indices[None, :] % length
    angles = residue.astype(jnp.float32) * (2.0 * math.pi / length)
    return (jnp.cos(angles), jnp.sin(angles))


def kernel_block(length, y_offset, y_count):
    indices = jnp.arange(length, dtype=jnp.int32)
    signed = jnp.where(indices < length // 2, indices, indices - length).astype(jnp.float32)
    wavenum = signed * (2.0 * math.pi / length)
    y_indices = y_offset + jnp.arange(y_count, dtype=jnp.int32)
    y_signed = jnp.where(y_indices < length // 2, y_indices, y_indices - length).astype(jnp.float32)
    y_wavenum = y_signed * (2.0 * math.pi / length)
    squares = (
        wavenum[:, None, None] ** 2 + y_wavenum[None, :, None] ** 2 + wavenum[None, None, :] ** 2
    )
    guarded = jnp.where(squares > 0, squares, 1.0)
    kernel = jnp.where(
        squares > 0, (1.0 - jnp.exp(-guarded / (4.0 * SCREEN * SCREEN))) / guarded, 0.0
    )
    kernel = kernel / float(length) ** 3
    return jnp.concatenate([kernel, kernel], -1)


def along_axis(spectrum, dimension, cosine_table, sine_table, direction):
    halfway = spectrum.shape[-1] // 2
    if dimension == 1:
        formula = "nakm,ab->nbkm"
    else:
        formula = "nakm,kb->nabm"
    cos_part = jnp.einsum(formula, spectrum, cosine_table, precision=lax.Precision.HIGH)
    sin_part = jnp.einsum(formula, spectrum, sine_table, precision=lax.Precision.HIGH)
    rotated = jnp.concatenate([-sin_part[..., halfway:], sin_part[..., :halfway]], -1)
    return cos_part + direction * rotated


def along_z(fields, cosine_table, sine_table, direction):
    top = jnp.concatenate([cosine_table, direction * sine_table], 1)
    bottom = jnp.concatenate([-direction * sine_table, cosine_table], 1)
    matrix = jnp.concatenate([top, bottom], 0)
    return jnp.einsum("nayz,zc->nayc", fields, matrix, precision=lax.Precision.HIGH)


def fetch_sources(orbitals, same_core):
    pieces = orbitals.reshape(2, 8, 32, 128).transpose(0, 2, 1, 3).reshape(CHIPS, 4, 8, 128)
    spread = lax.all_to_all(pieces, "band", 0, 0, axis_index_groups=same_core, tiled=True)
    mine = jnp.broadcast_to(spread[:1], (CHIPS, 4, 8, 128))
    whole = lax.all_to_all(mine, "band", 0, 0, axis_index_groups=same_core, tiled=True)
    return whole.reshape(2, 32, 8, 128)


def per_device(orbitals):
    owned, planes, flat_cells = orbitals.shape
    length = GRID
    same_core = [[b for b in range(32) if b % 2 == c] for c in (0, 1)]
    first = fetch_sources(orbitals, same_core)
    second = lax.ppermute(first, "band", [(b, b ^ 1) for b in range(32)])
    cosine_table, sine_table = angle_tables(length)
    kernel_slab = kernel_block(length, lax.axis_index("fft") * planes, planes)
    cells = orbitals.reshape(owned, planes, length, length)
    accumulated = jnp.zeros((owned, planes, length, length), jnp.float32)
    for sources in (first, second):
        sources = sources.transpose(0, 2, 1, 3).reshape(2, planes, length, length)
        density = jnp.concatenate([cells * sources[0], cells * sources[1]], -1)
        spectrum = along_z(density, cosine_table, sine_table, -1.0)
        spectrum = along_axis(spectrum, 2, cosine_table, sine_table, -1.0)
        spectrum = lax.all_to_all(spectrum, "fft", split_axis=2, concat_axis=1, tiled=True)
        filtered = along_axis(spectrum, 1, cosine_table, sine_table, -1.0) * kernel_slab
        filtered = along_axis(filtered, 1, cosine_table, sine_table, 1.0)
        returned = lax.all_to_all(filtered, "fft", split_axis=1, concat_axis=2, tiled=True)
        potential = along_axis(returned, 2, cosine_table, sine_table, 1.0)
        potential = along_z(potential, cosine_table, sine_table, 1.0)
        accumulated = accumulated + potential[..., :length] * sources[0]
        accumulated = accumulated + potential[..., length:] * sources[1]
    return (-EXX_FRACTION * accumulated).reshape(owned, planes, flat_cells)


def solution(mesh):
    return jax.shard_map(
        per_device,
        mesh=mesh,
        in_specs=(P("band", "fft", None),),
        out_specs=P("band", "fft", None),
        check_vma=False,
    )
```

```python
import functools
import math

import jax
import jax.numpy as jnp
import numpy as np
from jax import lax
from jax.experimental import pallas as pl
from jax.experimental.pallas import tpu as pltpu
from jax.sharding import PartitionSpec as P

GRID = 64
EXX_FRACTION = 0.25
SCREEN = 0.05
CHIPS = 16
PLANES = 8
LANES = 128


def split_table(table):
    high = np.asarray(table, np.float32).astype(jnp.bfloat16)
    low = (table - high.astype(np.float64)).astype(np.float32).astype(jnp.bfloat16)
    return high, low


def left_table(direction):
    index = np.arange(GRID)
    angles = (index[:, None] * index[None, :] % GRID) * (2.0 * math.pi / GRID)
    cosine, sine = np.cos(angles), direction * np.sin(angles)
    high, low = split_table(np.block([[cosine, -sine], [sine, cosine]]))
    return np.concatenate([high, high, low], 1)


def right_table(direction):
    index = np.arange(GRID)
    angles = (index[:, None] * index[None, :] % GRID) * (2.0 * math.pi / GRID)
    cosine, sine = np.cos(angles), direction * np.sin(angles)
    pair = np.eye(2)
    table = np.block(
        [
            [np.kron(pair, cosine), np.kron(pair, sine)],
            [np.kron(pair, -sine), np.kron(pair, cosine)],
        ]
    )
    high, low = split_table(table)
    return np.concatenate([high, high, low], 0)


def filter_table(y_offset):
    indices = jnp.arange(GRID, dtype=jnp.int32)
    signed = jnp.where(indices < GRID // 2, indices, indices - GRID).astype(jnp.float32)
    wavenum = signed * (2.0 * math.pi / GRID)
    y_indices = y_offset + jnp.arange(PLANES, dtype=jnp.int32)
    y_signed = jnp.where(y_indices < GRID // 2, y_indices, y_indices - GRID).astype(jnp.float32)
    y_wavenum = y_signed * (2.0 * math.pi / GRID)
    wide = jnp.concatenate([wavenum, wavenum])
    squares = wavenum[None, :, None] ** 2 + y_wavenum[:, None, None] ** 2 + wide[None, None, :] ** 2
    guarded = jnp.where(squares > 0, squares, 1.0)
    kernel = jnp.where(
        squares > 0, (1.0 - jnp.exp(-guarded / (4.0 * SCREEN * SCREEN))) / guarded, 0.0
    )
    return kernel * (-EXX_FRACTION / float(GRID) ** 3)


def parts(values):
    high = values.astype(jnp.bfloat16)
    low = (values - high.astype(jnp.float32)).astype(jnp.bfloat16)
    return high, low


def times_left(table, values):
    high, low = parts(values)
    stacked = jnp.concatenate([high, low, high], 0)
    return jnp.dot(table, stacked, preferred_element_type=jnp.float32)


def times_right(values, table):
    high, low = parts(values)
    stacked = jnp.concatenate([high, low, high], 1)
    return jnp.dot(stacked, table, preferred_element_type=jnp.float32)


def pair_sources(own_ref, other_ref, part, y_half, low_lanes):
    own, other = own_ref[part, y_half], other_ref[part, y_half]
    even = jnp.where(low_lanes, own, pltpu.roll(other, GRID, 1))
    odd = jnp.where(low_lanes, pltpu.roll(own, GRID, 1), other)
    return even, odd


def forward_kernel(orb_ref, own_ref, other_ref, right_ref, left_ref, out_ref, pair_ref, work_ref):
    low_lanes = lax.broadcasted_iota(jnp.int32, (PLANES, LANES), 1) < GRID
    for y_half in range(GRID // 2):
        for part in range(2):
            even, odd = pair_sources(own_ref, other_ref, part, y_half, low_lanes)
            for i in range(2):
                tile = orb_ref[i, :, y_half * LANES : (y_half + 1) * LANES]
                turned = pltpu.roll(tile, GRID, 1)
                base = y_half * 2 * PLANES
                lanes = slice(part * LANES, (part + 1) * LANES)
                pair_ref[i, base : base + PLANES, lanes] = (
                    jnp.where(low_lanes, tile, turned) * even
                )
                pair_ref[i, base + PLANES : base + 2 * PLANES, lanes] = (
                    jnp.where(low_lanes, turned, tile) * odd
                )
    for i in range(2):
        result = times_right(pair_ref[i], right_ref[...])
        work_ref[0] = result[:, :LANES]
        work_ref[1] = result[:, LANES:]
        for x in range(0, PLANES, 2):
            columns = []
            for plane in (x, x + 1):
                rows = [work_ref[part, pl.ds(plane, GRID, stride=PLANES), :] for part in range(2)]
                columns.append(jnp.concatenate(rows, 0))
            result = times_left(left_ref[...], jnp.concatenate(columns, 1))
            for k in range(2):
                for part in range(2):
                    block = result[part * GRID : (part + 1) * GRID, k * LANES : (k + 1) * LANES]
                    out_ref[:, i, x + k, part] = block.reshape(8, PLANES, LANES)


def middle_kernel(in_ref, forth_ref, back_ref, filter_ref, out_ref):
    for i in range(2):
        for ky in range(0, PLANES, 2):
            columns = []
            for y in (ky, ky + 1):
                rows = []
                for part in range(2):
                    for block in range(8):
                        start = block * 256 + i * 128 + part * 8 + y
                        rows.append(in_ref[pl.ds(start, PLANES, stride=16), :])
                columns.append(jnp.concatenate(rows, 0))
            spectrum = times_left(forth_ref[...], jnp.concatenate(columns, 1))
            scale = jnp.concatenate([filter_ref[ky], filter_ref[ky + 1]], 1)
            spectrum = spectrum * jnp.concatenate([scale, scale], 0)
            result = times_left(back_ref[...], spectrum)
            for k in range(2):
                for part in range(2):
                    for block in range(8):
                        start = block * 256 + i * 128 + part * 8 + ky + k
                        top = part * GRID + block * PLANES
                        out_ref[pl.ds(start, PLANES, stride=16), :] = result[
                            top : top + PLANES, k * LANES : (k + 1) * LANES
                        ]


def inverse_kernel(in_ref, own_ref, other_ref, right_ref, left_ref, out_ref, work_ref):
    low_lanes = lax.broadcasted_iota(jnp.int32, (PLANES, LANES), 1) < GRID
    for i in range(2):
        for x in range(0, PLANES, 2):
            columns = []
            for plane in (x, x + 1):
                rows = [in_ref[:, i, plane, part].reshape(GRID, LANES) for part in range(2)]
                columns.append(jnp.concatenate(rows, 0))
            result = times_left(left_ref[...], jnp.concatenate(columns, 1))
            for k in range(2):
                for part in range(2):
                    work_ref[part, pl.ds(x + k, GRID, stride=PLANES), :] = result[
                        part * GRID : (part + 1) * GRID, k * LANES : (k + 1) * LANES
                    ]
        potential = times_right(jnp.concatenate([work_ref[0], work_ref[1]], 1), right_ref[...])
        for y_half in range(GRID // 2):
            sums = [0.0, 0.0]
            for part in range(2):
                pair = pair_sources(own_ref, other_ref, part, y_half, low_lanes)
                for odd in range(2):
                    base = (y_half * 2 + odd) * PLANES
                    values = potential[base : base + PLANES, part * LANES : (part + 1) * LANES]
                    sums[odd] = sums[odd] + values * pair[odd]
            even, odd = (s + pltpu.roll(s, GRID, 1) for s in sums)
            out_ref[i, :, y_half * LANES : (y_half + 1) * LANES] = jnp.where(low_lanes, even, odd)


def local_call(kernel, shape, scratch):
    return pl.pallas_call(
        kernel,
        out_shape=jax.ShapeDtypeStruct(shape, jnp.float32),
        scratch_shapes=scratch,
        compiler_params=pltpu.CompilerParams(vmem_limit_bytes=24 << 20),
    )


def fetch_sources(orbitals, same_core):
    pieces = orbitals.reshape(2, 8, 32, 128).transpose(0, 2, 1, 3).reshape(CHIPS, 4, 8, 128)
    spread = lax.all_to_all(pieces, "band", 0, 0, axis_index_groups=same_core, tiled=True)
    mine = jnp.broadcast_to(spread[:1], (CHIPS, 4, 8, 128))
    whole = lax.all_to_all(mine, "band", 0, 0, axis_index_groups=same_core, tiled=True)
    return whole.reshape(2, 32, 8, 128)


def per_device(orbitals):
    same_core = [[b for b in range(32) if b % 2 == c] for c in (0, 1)]
    own = fetch_sources(orbitals, same_core)
    other = lax.ppermute(own, "band", [(b, b ^ 1) for b in range(32)])
    filters = filter_table(lax.axis_index("fft") * PLANES)
    left_forth, left_back = (jnp.asarray(left_table(s)) for s in (-1.0, 1.0))
    right_forth, right_back = (jnp.asarray(right_table(s)) for s in (-1.0, 1.0))
    rows = PLANES * GRID
    work = pltpu.VMEM((2, rows, LANES), jnp.float32)
    spectrum = local_call(
        forward_kernel,
        (8, 2, PLANES, 2, PLANES, LANES),
        [pltpu.VMEM((2, rows, 2 * LANES), jnp.float32), work],
    )(orbitals, own, other, right_forth, left_forth)
    spectrum = lax.all_to_all(spectrum, "fft", 0, 0, tiled=True)
    filtered = local_call(middle_kernel, (2048, LANES), [])(
        spectrum.reshape(2048, LANES), left_forth, left_back, filters
    )
    filtered = filtered.reshape(8, 2, PLANES, 2, PLANES, LANES)
    returned = lax.all_to_all(filtered, "fft", 0, 0, tiled=True)
    return local_call(inverse_kernel, (2, PLANES, GRID * GRID), [work])(
        returned, own, other, right_back, left_back
    )


def solution(mesh):
    return jax.shard_map(
        per_device,
        mesh=mesh,
        in_specs=(P("band", "fft", None),),
        out_specs=P("band", "fft", None),
        check_vma=False,
    )
```

```python
import math

import jax
import jax.numpy as jnp
from jax import lax
from jax.experimental import pallas as pl
from jax.experimental.pallas import tpu as pltpu
from jax.sharding import PartitionSpec as P


GRID = 64
EXX_FRACTION = 0.25
SCREEN = 0.05
CHIPS = 16
PLANES = 8
LANES = 128


ORDER = (6, 7, 5, 4, 2, 3, 1)


def split_table(table, axis):
    high = lax.reduce_precision(table, 8, 7)
    return jnp.concatenate([high, high, table - high], axis).astype(jnp.bfloat16)


def wave(rows, columns, direction):
    angles = (rows[:, None] * columns[None, :] % GRID).astype(jnp.float32) * (2.0 * math.pi / GRID)
    return jnp.cos(angles), direction * jnp.sin(angles)


def left_table(rows, columns, direction):
    cosine, sine = wave(rows, columns, direction)
    top = jnp.concatenate([cosine, -sine], 1)
    bottom = jnp.concatenate([sine, cosine], 1)
    return split_table(jnp.concatenate([top, bottom], 0), 1)


def right_table(direction):
    index = jnp.arange(GRID, dtype=jnp.int32)
    cosine, sine = wave(index, index, direction)
    zero = jnp.zeros_like(cosine)
    table = jnp.concatenate(
        [
            jnp.concatenate([cosine, zero, sine, zero], 1),
            jnp.concatenate([zero, cosine, zero, sine], 1),
            jnp.concatenate([-sine, zero, cosine, zero], 1),
            jnp.concatenate([zero, -sine, zero, cosine], 1),
        ],
        0,
    )
    return split_table(table, 0)


def filter_table(y_offset):
    indices = jnp.arange(GRID, dtype=jnp.int32)
    signed = jnp.where(indices < GRID // 2, indices, indices - GRID).astype(jnp.float32)
    wavenum = signed * (2.0 * math.pi / GRID)
    y_indices = y_offset + jnp.arange(PLANES, dtype=jnp.int32)
    y_signed = jnp.where(y_indices < GRID // 2, y_indices, y_indices - GRID).astype(jnp.float32)
    y_wavenum = y_signed * (2.0 * math.pi / GRID)
    wide = jnp.concatenate([wavenum, wavenum])
    squares = wavenum[None, :, None] ** 2 + y_wavenum[:, None, None] ** 2 + wide[None, None, :] ** 2
    guarded = jnp.where(squares > 0, squares, 1.0)
    kernel = jnp.where(
        squares > 0, (1.0 - jnp.exp(-guarded / (4.0 * SCREEN * SCREEN))) / guarded, 0.0
    )
    return kernel * (-EXX_FRACTION / float(GRID) ** 3)


def parts(values):
    high = values.astype(jnp.bfloat16)
    low = (values - high.astype(jnp.float32)).astype(jnp.bfloat16)
    return high, low


def times_left(table, values):
    high, low = parts(values)
    stacked = jnp.concatenate([high, low, high], 0)
    return jnp.dot(table, stacked, preferred_element_type=jnp.float32)


def times_right(values, table):
    high, low = parts(values)
    stacked = jnp.concatenate([high, low, high], 1)
    return jnp.dot(stacked, table, preferred_element_type=jnp.float32)


def pair_sources(own_ref, other_ref, part, y_half, low_lanes):
    own, other = own_ref[part, y_half], other_ref[part, y_half]
    even = jnp.where(low_lanes, own, pltpu.roll(other, GRID, 1))
    odd = jnp.where(low_lanes, pltpu.roll(own, GRID, 1), other)
    return even, odd


def forward_kernel(orb_ref, own_ref, other_ref, right_ref, left_ref, *refs):
    out_refs, (pair_ref, work_ref) = refs[:8], refs[8:]
    low_lanes = lax.broadcasted_iota(jnp.int32, (PLANES, LANES), 1) < GRID
    for y_half in range(GRID // 2):
        for part in range(2):
            even, odd = pair_sources(own_ref, other_ref, part, y_half, low_lanes)
            for i in range(2):
                tile = orb_ref[i, :, y_half * LANES : (y_half + 1) * LANES]
                turned = pltpu.roll(tile, GRID, 1)
                base = y_half * 2 * PLANES
                lanes = slice(part * LANES, (part + 1) * LANES)
                pair_ref[i, base : base + PLANES, lanes] = (
                    jnp.where(low_lanes, tile, turned) * even
                )
                pair_ref[i, base + PLANES : base + 2 * PLANES, lanes] = (
                    jnp.where(low_lanes, turned, tile) * odd
                )
    for i in range(2):
        result = times_right(pair_ref[i], right_ref[...])
        work_ref[0] = result[:, :LANES]
        work_ref[1] = result[:, LANES:]
        for x in range(0, PLANES, 2):
            columns = []
            for plane in (x, x + 1):
                rows = [work_ref[part, pl.ds(plane, GRID, stride=PLANES), :] for part in range(2)]
                columns.append(jnp.concatenate(rows, 0))
            result = times_left(left_ref[...], jnp.concatenate(columns, 1))
            for k in range(2):
                for part in range(2):
                    for block in range(8):
                        top = part * GRID + block * PLANES
                        out_refs[block][i, x + k, part] = result[
                            top : top + PLANES, k * LANES : (k + 1) * LANES
                        ]


def middle_kernel(*refs):
    in_refs, (forth_ref, back_ref, filter_ref), out_refs = refs[:8], refs[8:11], refs[11:]
    for i in range(2):
        for ky in range(0, PLANES, 2):
            columns = []
            for y in (ky, ky + 1):
                rows = []
                for part in range(2):
                    for block in range(8):
                        start = i * 128 + part * 8 + y
                        rows.append(in_refs[block][pl.ds(start, PLANES, stride=16), :])
                columns.append(jnp.concatenate(rows, 0))
            spectrum = times_left(forth_ref[...], jnp.concatenate(columns, 1))
            scale = jnp.concatenate([filter_ref[ky], filter_ref[ky + 1]], 1)
            spectrum = spectrum * jnp.concatenate([scale, scale], 0)
            result = times_left(back_ref[...], spectrum)
            for k in range(2):
                for part in range(2):
                    for block in range(8):
                        start = i * 128 + part * 8 + ky + k
                        top = part * GRID + block * PLANES
                        out_refs[block][pl.ds(start, PLANES, stride=16), :] = result[
                            top : top + PLANES, k * LANES : (k + 1) * LANES
                        ]


def inverse_kernel(*refs):
    in_refs, (own_ref, other_ref, right_ref, left_ref, out_ref, work_ref) = refs[:8], refs[8:]
    low_lanes = lax.broadcasted_iota(jnp.int32, (PLANES, LANES), 1) < GRID
    for i in range(2):
        for x in range(0, PLANES, 2):
            columns = []
            for plane in (x, x + 1):
                rows = [ref[i, plane, part] for part in range(2) for ref in in_refs]
                columns.append(jnp.concatenate(rows, 0))
            result = times_left(left_ref[...], jnp.concatenate(columns, 1))
            for k in range(2):
                for part in range(2):
                    work_ref[part, pl.ds(x + k, GRID, stride=PLANES), :] = result[
                        part * GRID : (part + 1) * GRID, k * LANES : (k + 1) * LANES
                    ]
        potential = times_right(jnp.concatenate([work_ref[0], work_ref[1]], 1), right_ref[...])
        for y_half in range(GRID // 2):
            sums = [0.0, 0.0]
            for part in range(2):
                pair = pair_sources(own_ref, other_ref, part, y_half, low_lanes)
                for odd in range(2):
                    base = (y_half * 2 + odd) * PLANES
                    values = potential[base : base + PLANES, part * LANES : (part + 1) * LANES]
                    sums[odd] = sums[odd] + values * pair[odd]
            even, odd = (s + pltpu.roll(s, GRID, 1) for s in sums)
            out_ref[i, :, y_half * LANES : (y_half + 1) * LANES] = jnp.where(low_lanes, even, odd)


def local_call(kernel, shapes, scratch):
    return pl.pallas_call(
        kernel,
        out_shape=[jax.ShapeDtypeStruct(shape, jnp.float32) for shape in shapes],
        scratch_shapes=scratch,
        compiler_params=pltpu.CompilerParams(vmem_limit_bytes=24 << 20),
    )


def fetch_sources(orbitals, same_core):
    pieces = orbitals.reshape(2, 8, 32, 128).transpose(0, 2, 1, 3).reshape(CHIPS, 4, 8, 128)
    spread = lax.all_to_all(pieces, "band", 0, 0, axis_index_groups=same_core, tiled=True)
    mine = jnp.broadcast_to(spread[:1], (CHIPS, 4, 8, 128))
    whole = lax.all_to_all(mine, "band", 0, 0, axis_index_groups=same_core, tiled=True)
    return whole.reshape(2, 32, 8, 128)


def exchange(blocks):
    results = list(blocks)
    for d in ORDER:
        results[d] = lax.ppermute(blocks[d], "fft", [(p, p ^ d) for p in range(8)])
    return results


def per_device(orbitals):
    same_core = [[b for b in range(32) if b % 2 == c] for c in (0, 1)]
    own = fetch_sources(orbitals, same_core)
    other = lax.ppermute(own, "band", [(b, b ^ 1) for b in range(32)])
    here = lax.axis_index("fft")
    filters = filter_table(here * PLANES)
    index = jnp.arange(GRID, dtype=jnp.int32)
    mixed = (index // PLANES ^ here) * PLANES + index % PLANES
    right_forth, right_back = right_table(-1.0), right_table(1.0)
    rows = PLANES * GRID
    work = pltpu.VMEM((2, rows, LANES), jnp.float32)
    block = (2, PLANES, 2, PLANES, LANES)
    flat = (2 * PLANES * 2 * PLANES, LANES)
    spectrum = local_call(
        forward_kernel,
        [block] * 8,
        [pltpu.VMEM((2, rows, 2 * LANES), jnp.float32), work],
    )(orbitals, own, other, right_forth, left_table(mixed, index, -1.0))
    spectrum = [a.reshape(flat) for a in exchange(spectrum)]
    filtered = local_call(middle_kernel, [flat] * 8, [])(
        *spectrum, left_table(index, mixed, -1.0), left_table(mixed, index, 1.0), filters
    )
    returned = exchange([a.reshape(block) for a in filtered])
    return local_call(inverse_kernel, [(2, PLANES, GRID * GRID)], [work])(
        *returned, own, other, right_back, left_table(index, mixed, 1.0)
    )[0]


def solution(mesh):
    return jax.shard_map(
        per_device,
        mesh=mesh,
        in_specs=(P("band", "fft", None),),
        out_specs=P("band", "fft", None),
        check_vma=False,
    )
```

```python
import math

import jax
import jax.numpy as jnp
from jax import lax
from jax.experimental import pallas as pl
from jax.experimental.pallas import tpu as pltpu
from jax.sharding import PartitionSpec as P


GRID = 64
EXX_FRACTION = 0.25
SCREEN = 0.05
PLANES = 8
LANES = 128


ORDER = (6, 7, 5, 4, 2, 3, 1)
REACH = (4, 3, 5, 2, 6, 1, 7)


def split_table(table, axis):
    high = lax.reduce_precision(table, 8, 7)
    return jnp.concatenate([high, high, table - high], axis).astype(jnp.bfloat16)


def wave(rows, columns, direction):
    angles = (rows[:, None] * columns[None, :] % GRID).astype(jnp.float32) * (2.0 * math.pi / GRID)
    return jnp.cos(angles), direction * jnp.sin(angles)


def left_table(rows, columns, direction):
    cosine, sine = wave(rows, columns, direction)
    top = jnp.concatenate([cosine, -sine], 1)
    bottom = jnp.concatenate([sine, cosine], 1)
    return split_table(jnp.concatenate([top, bottom], 0), 1)


def right_table(direction):
    index = jnp.arange(GRID, dtype=jnp.int32)
    cosine, sine = wave(index, index, direction)
    zero = jnp.zeros_like(cosine)
    table = jnp.concatenate(
        [
            jnp.concatenate([cosine, zero, sine, zero], 1),
            jnp.concatenate([zero, cosine, zero, sine], 1),
            jnp.concatenate([-sine, zero, cosine, zero], 1),
            jnp.concatenate([zero, -sine, zero, cosine], 1),
        ],
        0,
    )
    return split_table(table, 0)


def filter_table(y_offset):
    indices = jnp.arange(GRID, dtype=jnp.int32)
    signed = jnp.where(indices < GRID // 2, indices, indices - GRID).astype(jnp.float32)
    wavenum = signed * (2.0 * math.pi / GRID)
    y_indices = y_offset + jnp.arange(PLANES, dtype=jnp.int32)
    y_signed = jnp.where(y_indices < GRID // 2, y_indices, y_indices - GRID).astype(jnp.float32)
    y_wavenum = y_signed * (2.0 * math.pi / GRID)
    wide = jnp.concatenate([wavenum, wavenum])
    squares = wavenum[None, :, None] ** 2 + y_wavenum[:, None, None] ** 2 + wide[None, None, :] ** 2
    guarded = jnp.where(squares > 0, squares, 1.0)
    kernel = jnp.where(
        squares > 0, (1.0 - jnp.exp(-guarded / (4.0 * SCREEN * SCREEN))) / guarded, 0.0
    )
    return kernel * (-EXX_FRACTION / float(GRID) ** 3)


def parts(values):
    high = values.astype(jnp.bfloat16)
    low = (values - high.astype(jnp.float32)).astype(jnp.bfloat16)
    return high, low


def times_left(table, values):
    high, low = parts(values)
    stacked = jnp.concatenate([high, low, high], 0)
    return jnp.dot(table, stacked, preferred_element_type=jnp.float32)


def times_right(values, table):
    high, low = parts(values)
    stacked = jnp.concatenate([high, low, high], 1)
    return jnp.dot(stacked, table, preferred_element_type=jnp.float32)


def pair_sources(own_refs, other_refs, part, y_half, low_lanes):
    columns = slice(y_half * LANES, (y_half + 1) * LANES)
    own, other = own_refs[part][:, columns], other_refs[part][:, columns]
    even = jnp.where(low_lanes, own, pltpu.roll(other, GRID, 1))
    odd = jnp.where(low_lanes, pltpu.roll(own, GRID, 1), other)
    return even, odd


def forward_kernel(orb_ref, *refs):
    own_refs, other_refs, (right_ref, left_ref) = refs[:2], refs[2:4], refs[4:6]
    out_refs, (pair_ref, work_ref) = refs[6:14], refs[14:]
    low_lanes = lax.broadcasted_iota(jnp.int32, (PLANES, LANES), 1) < GRID
    for y_half in range(GRID // 2):
        for part in range(2):
            even, odd = pair_sources(own_refs, other_refs, part, y_half, low_lanes)
            for i in range(2):
                tile = orb_ref[i, :, y_half * LANES : (y_half + 1) * LANES]
                turned = pltpu.roll(tile, GRID, 1)
                base = y_half * 2 * PLANES
                lanes = slice(part * LANES, (part + 1) * LANES)
                pair_ref[i, base : base + PLANES, lanes] = (
                    jnp.where(low_lanes, tile, turned) * even
                )
                pair_ref[i, base + PLANES : base + 2 * PLANES, lanes] = (
                    jnp.where(low_lanes, turned, tile) * odd
                )
    for i in range(2):
        result = times_right(pair_ref[i], right_ref[...])
        work_ref[0] = result[:, :LANES]
        work_ref[1] = result[:, LANES:]
        for x in range(0, PLANES, 2):
            columns = []
            for plane in (x, x + 1):
                rows = [work_ref[part, pl.ds(plane, GRID, stride=PLANES), :] for part in range(2)]
                columns.append(jnp.concatenate(rows, 0))
            result = times_left(left_ref[...], jnp.concatenate(columns, 1))
            for k in range(2):
                for part in range(2):
                    for block in range(8):
                        top = part * GRID + block * PLANES
                        out_refs[block][i, x + k, part] = result[
                            top : top + PLANES, k * LANES : (k + 1) * LANES
                        ]


def middle_kernel(*refs):
    in_refs, (forth_ref, back_ref, filter_ref), out_refs = refs[:8], refs[8:11], refs[11:]
    for i in range(2):
        for ky in range(0, PLANES, 2):
            columns = []
            for y in (ky, ky + 1):
                rows = []
                for part in range(2):
                    for block in range(8):
                        start = i * 128 + part * 8 + y
                        rows.append(in_refs[block][pl.ds(start, PLANES, stride=16), :])
                columns.append(jnp.concatenate(rows, 0))
            spectrum = times_left(forth_ref[...], jnp.concatenate(columns, 1))
            scale = jnp.concatenate([filter_ref[ky], filter_ref[ky + 1]], 1)
            spectrum = spectrum * jnp.concatenate([scale, scale], 0)
            result = times_left(back_ref[...], spectrum)
            for k in range(2):
                for part in range(2):
                    for block in range(8):
                        start = i * 128 + part * 8 + ky + k
                        top = part * GRID + block * PLANES
                        out_refs[block][pl.ds(start, PLANES, stride=16), :] = result[
                            top : top + PLANES, k * LANES : (k + 1) * LANES
                        ]


def inverse_kernel(*refs):
    in_refs, own_refs, other_refs = refs[:8], refs[8:10], refs[10:12]
    right_ref, left_ref, out_ref, work_ref = refs[12:]
    low_lanes = lax.broadcasted_iota(jnp.int32, (PLANES, LANES), 1) < GRID
    for i in range(2):
        for x in range(0, PLANES, 2):
            columns = []
            for plane in (x, x + 1):
                rows = [ref[i, plane, part] for part in range(2) for ref in in_refs]
                columns.append(jnp.concatenate(rows, 0))
            result = times_left(left_ref[...], jnp.concatenate(columns, 1))
            for k in range(2):
                for part in range(2):
                    work_ref[part, pl.ds(x + k, GRID, stride=PLANES), :] = result[
                        part * GRID : (part + 1) * GRID, k * LANES : (k + 1) * LANES
                    ]
        potential = times_right(jnp.concatenate([work_ref[0], work_ref[1]], 1), right_ref[...])
        for y_half in range(GRID // 2):
            sums = [0.0, 0.0]
            for part in range(2):
                pair = pair_sources(own_refs, other_refs, part, y_half, low_lanes)
                for odd in range(2):
                    base = (y_half * 2 + odd) * PLANES
                    values = potential[base : base + PLANES, part * LANES : (part + 1) * LANES]
                    sums[odd] = sums[odd] + values * pair[odd]
            even, odd = (s + pltpu.roll(s, GRID, 1) for s in sums)
            out_ref[i, :, y_half * LANES : (y_half + 1) * LANES] = jnp.where(low_lanes, even, odd)


def local_call(kernel, shapes, scratch):
    return pl.pallas_call(
        kernel,
        out_shape=[jax.ShapeDtypeStruct(shape, jnp.float32) for shape in shapes],
        scratch_shapes=scratch,
        compiler_params=pltpu.CompilerParams(vmem_limit_bytes=24 << 20),
    )


def band_of(x_half, z, core):
    return x_half * 16 + z * 2 + core


def fetch_sources(orbitals):
    cores = (0, 1)
    band = lax.axis_index("band")
    x_half, z = band // 16, band // 2 % 8
    handed = lax.ppermute(
        orbitals[1], "band", [(band_of(0, 0, c), band_of(1, 0, c)) for c in cores]
    )
    root = jnp.where(x_half == 1, handed, orbitals[0])
    first = root
    for step in REACH:
        pairs = [(band_of(h, 0, c), band_of(h, step, c)) for h in cores for c in cores]
        first = jnp.where(z == step, lax.ppermute(root, "band", pairs), first)
    second = lax.ppermute(first, "band", [(b, b ^ 16) for b in range(32)])
    own = (first, second)
    other = tuple(lax.ppermute(a, "band", [(b, b ^ 1) for b in range(32)]) for a in own)
    return own, other


def exchange(blocks):
    results = list(blocks)
    for d in ORDER:
        results[d] = lax.ppermute(blocks[d], "fft", [(p, p ^ d) for p in range(8)])
    return results


def apply_exchange(orbitals):
    own, other = fetch_sources(orbitals)
    here = lax.axis_index("fft")
    filters = filter_table(here * PLANES)
    index = jnp.arange(GRID, dtype=jnp.int32)
    mixed = (index // PLANES ^ here) * PLANES + index % PLANES
    right_forth, right_back = right_table(-1.0), right_table(1.0)
    rows = PLANES * GRID
    work = pltpu.VMEM((2, rows, LANES), jnp.float32)
    block = (2, PLANES, 2, PLANES, LANES)
    flat = (2 * PLANES * 2 * PLANES, LANES)
    spectrum = local_call(
        forward_kernel,
        [block] * 8,
        [pltpu.VMEM((2, rows, 2 * LANES), jnp.float32), work],
    )(orbitals, *own, *other, right_forth, left_table(mixed, index, -1.0))
    spectrum = [a.reshape(flat) for a in exchange(spectrum)]
    filtered = local_call(middle_kernel, [flat] * 8, [])(
        *spectrum, left_table(index, mixed, -1.0), left_table(mixed, index, 1.0), filters
    )
    returned = exchange([a.reshape(block) for a in filtered])
    return local_call(inverse_kernel, [(2, PLANES, GRID * GRID)], [work])(
        *returned, *own, *other, right_back, left_table(index, mixed, 1.0)
    )[0]


def solution(mesh):
    return jax.shard_map(
        apply_exchange,
        mesh=mesh,
        in_specs=(P("band", "fft", None),),
        out_specs=P("band", "fft", None),
        check_vma=False,
    )
```

```python
import math

import jax
import jax.numpy as jnp
from jax import lax
from jax.experimental import pallas as pl
from jax.experimental.pallas import tpu as pltpu
from jax.sharding import PartitionSpec as P


GRID = 64
EXX_FRACTION = 0.25
SCREEN = 0.05
PLANES = 8
LANES = 128


ORDER = (2, 6, 4, 7, 5, 3, 1)
REACH = (4, 3, 5, 2, 6, 1, 7)


def split_table(table, axis):
    high = lax.reduce_precision(table, 8, 7)
    return jnp.concatenate([high, high, table - high], axis).astype(jnp.bfloat16)


def wave(rows, columns, direction):
    angles = (rows[:, None] * columns[None, :] % GRID).astype(jnp.float32) * (2.0 * math.pi / GRID)
    return jnp.cos(angles), direction * jnp.sin(angles)


def left_table(rows, columns, direction):
    cosine, sine = wave(rows, columns, direction)
    top = jnp.concatenate([cosine, -sine], 1)
    bottom = jnp.concatenate([sine, cosine], 1)
    return split_table(jnp.concatenate([top, bottom], 0), 1)


def right_table(index, direction):
    cosine, sine = wave(index, index, direction)
    zero = jnp.zeros_like(cosine)
    table = jnp.concatenate(
        [
            jnp.concatenate([cosine, zero, sine, zero], 1),
            jnp.concatenate([zero, cosine, zero, sine], 1),
            jnp.concatenate([-sine, zero, cosine, zero], 1),
            jnp.concatenate([zero, -sine, zero, cosine], 1),
        ],
        0,
    )
    return split_table(table, 0)


def filter_table(index, here):
    signed = jnp.where(index < GRID // 2, index, index - GRID).astype(jnp.float32)
    wavenum = signed * (2.0 * math.pi / GRID)
    y_indices = here * PLANES + index[:PLANES]
    y_signed = jnp.where(y_indices < GRID // 2, y_indices, y_indices - GRID).astype(jnp.float32)
    y_wavenum = y_signed * (2.0 * math.pi / GRID)
    wide = jnp.concatenate([wavenum, wavenum])
    squares = wavenum[None, :, None] ** 2 + y_wavenum[:, None, None] ** 2 + wide[None, None, :] ** 2
    guarded = jnp.where(squares > 0, squares, 1.0)
    kernel = jnp.where(
        squares > 0, (1.0 - jnp.exp(-guarded / (4.0 * SCREEN * SCREEN))) / guarded, 0.0
    )
    return kernel * (-EXX_FRACTION / float(GRID) ** 3)


def parts(values):
    high = values.astype(jnp.bfloat16)
    low = (values - high.astype(jnp.float32)).astype(jnp.bfloat16)
    return high, low


def times_left(table, values):
    high, low = parts(values)
    stacked = jnp.concatenate([high, low, high], 0)
    return jnp.dot(table, stacked, preferred_element_type=jnp.float32)


def times_right(values, table):
    high, low = parts(values)
    stacked = jnp.concatenate([high, low, high], 1)
    return jnp.dot(stacked, table, preferred_element_type=jnp.float32)


def pair_sources(own_refs, other_refs, part, y_half, low_lanes):
    columns = slice(y_half * LANES, (y_half + 1) * LANES)
    own, other = own_refs[part][:, columns], other_refs[part][:, columns]
    even = jnp.where(low_lanes, own, pltpu.roll(other, GRID, 1))
    odd = jnp.where(low_lanes, pltpu.roll(own, GRID, 1), other)
    return even, odd


def forward_kernel(orb_ref, *refs):
    own_refs, other_refs, (right_ref, left_ref) = refs[:2], refs[2:4], refs[4:6]
    out_refs, (pair_ref, work_ref) = refs[6:14], refs[14:]
    low_lanes = lax.broadcasted_iota(jnp.int32, (PLANES, LANES), 1) < GRID
    for y_half in range(GRID // 2):
        for part in range(2):
            even, odd = pair_sources(own_refs, other_refs, part, y_half, low_lanes)
            for i in range(2):
                tile = orb_ref[i, :, y_half * LANES : (y_half + 1) * LANES]
                turned = pltpu.roll(tile, GRID, 1)
                base = y_half * 2 * PLANES
                lanes = slice(part * LANES, (part + 1) * LANES)
                pair_ref[i, base : base + PLANES, lanes] = (
                    jnp.where(low_lanes, tile, turned) * even
                )
                pair_ref[i, base + PLANES : base + 2 * PLANES, lanes] = (
                    jnp.where(low_lanes, turned, tile) * odd
                )
    for i in range(2):
        result = times_right(pair_ref[i], right_ref[...])
        work_ref[0] = result[:, :LANES]
        work_ref[1] = result[:, LANES:]
        for x in range(0, PLANES, 2):
            columns = []
            for plane in (x, x + 1):
                rows = [work_ref[part, pl.ds(plane, GRID, stride=PLANES), :] for part in range(2)]
                columns.append(jnp.concatenate(rows, 0))
            result = times_left(left_ref[...], jnp.concatenate(columns, 1))
            for k in range(2):
                for part in range(2):
                    for block in range(8):
                        top = part * GRID + block * PLANES
                        out_refs[block][i, x + k, part] = result[
                            top : top + PLANES, k * LANES : (k + 1) * LANES
                        ]


def middle_kernel(*refs):
    in_refs, (forth_ref, back_ref, filter_ref), out_refs = refs[:8], refs[8:11], refs[11:]
    for i in range(2):
        for ky in range(0, PLANES, 2):
            columns = []
            for y in (ky, ky + 1):
                rows = []
                for part in range(2):
                    for block in range(8):
                        start = i * 128 + part * 8 + y
                        rows.append(in_refs[block][pl.ds(start, PLANES, stride=16), :])
                columns.append(jnp.concatenate(rows, 0))
            spectrum = times_left(forth_ref[...], jnp.concatenate(columns, 1))
            scale = jnp.concatenate([filter_ref[ky], filter_ref[ky + 1]], 1)
            spectrum = spectrum * jnp.concatenate([scale, scale], 0)
            result = times_left(back_ref[...], spectrum)
            for k in range(2):
                for part in range(2):
                    for block in range(8):
                        start = i * 128 + part * 8 + ky + k
                        top = part * GRID + block * PLANES
                        out_refs[block][pl.ds(start, PLANES, stride=16), :] = result[
                            top : top + PLANES, k * LANES : (k + 1) * LANES
                        ]


def inverse_kernel(*refs):
    in_refs, own_refs, other_refs = refs[:8], refs[8:10], refs[10:12]
    right_ref, left_ref, out_ref, work_ref = refs[12:]
    low_lanes = lax.broadcasted_iota(jnp.int32, (PLANES, LANES), 1) < GRID
    for i in range(2):
        for x in range(0, PLANES, 2):
            columns = []
            for plane in (x, x + 1):
                rows = [ref[i, plane, part] for part in range(2) for ref in in_refs]
                columns.append(jnp.concatenate(rows, 0))
            result = times_left(left_ref[...], jnp.concatenate(columns, 1))
            for k in range(2):
                for part in range(2):
                    work_ref[part, pl.ds(x + k, GRID, stride=PLANES), :] = result[
                        part * GRID : (part + 1) * GRID, k * LANES : (k + 1) * LANES
                    ]
        potential = times_right(jnp.concatenate([work_ref[0], work_ref[1]], 1), right_ref[...])
        for y_half in range(GRID // 2):
            sums = [0.0, 0.0]
            for part in range(2):
                pair = pair_sources(own_refs, other_refs, part, y_half, low_lanes)
                for odd in range(2):
                    base = (y_half * 2 + odd) * PLANES
                    values = potential[base : base + PLANES, part * LANES : (part + 1) * LANES]
                    sums[odd] = sums[odd] + values * pair[odd]
            even, odd = (s + pltpu.roll(s, GRID, 1) for s in sums)
            out_ref[i, :, y_half * LANES : (y_half + 1) * LANES] = jnp.where(low_lanes, even, odd)


def local_call(kernel, shapes, scratch):
    return pl.pallas_call(
        kernel,
        out_shape=[jax.ShapeDtypeStruct(shape, jnp.float32) for shape in shapes],
        scratch_shapes=scratch,
        compiler_params=pltpu.CompilerParams(vmem_limit_bytes=24 << 20),
    )


def band_of(x_half, z, core):
    return x_half * 16 + z * 2 + core


def fetch_sources(orbitals, here):
    cores = (0, 1)
    band = lax.axis_index("band")
    x_half, z = band // 16, band // 2 % 8
    handed = lax.ppermute(
        orbitals[1], "band", [(band_of(0, 0, c), band_of(1, 0, c)) for c in cores]
    )
    root = jnp.where(x_half == 1, handed, orbitals[0])
    first = root
    for step in REACH:
        pairs = [(band_of(h, 0, c), band_of(h, step, c)) for h in cores for c in cores]
        first = jnp.where(z == step, lax.ppermute(root, "band", pairs), first)
    index, mixed, first = indices_after(first, here)
    second = lax.ppermute(first, "band", [(b, b ^ 16) for b in range(32)])
    own = (first, second)
    other = tuple(lax.ppermute(a, "band", [(b, b ^ 1) for b in range(32)]) for a in own)
    return own, other, index, mixed


def exchange(blocks):
    results = list(blocks)
    for d in ORDER:
        results[d] = lax.ppermute(blocks[d], "fft", [(p, p ^ d) for p in range(8)])
    return results


def indices_after(value, here):
    index, value = lax.optimization_barrier((jnp.arange(GRID, dtype=jnp.int32), value))
    mixed = (index // PLANES ^ here) * PLANES + index % PLANES
    return index, mixed, value


def apply_exchange(orbitals):
    here = lax.axis_index("fft")
    own, other, index, mixed = fetch_sources(orbitals, here)
    rows = PLANES * GRID
    work = pltpu.VMEM((2, rows, LANES), jnp.float32)
    block = (2, PLANES, 2, PLANES, LANES)
    flat = (2 * PLANES * 2 * PLANES, LANES)
    spectrum = local_call(
        forward_kernel,
        [block] * 8,
        [pltpu.VMEM((2, rows, 2 * LANES), jnp.float32), work],
    )(orbitals, *own, *other, right_table(index, -1.0), left_table(mixed, index, -1.0))
    spectrum = exchange(spectrum)
    index, mixed, spectrum[ORDER[0]] = indices_after(spectrum[ORDER[0]], here)
    spectrum = [a.reshape(flat) for a in spectrum]
    filtered = local_call(middle_kernel, [flat] * 8, [])(
        *spectrum,
        left_table(index, mixed, -1.0),
        left_table(mixed, index, 1.0),
        filter_table(index, here),
    )
    returned = exchange([a.reshape(block) for a in filtered])
    index, mixed, returned[ORDER[0]] = indices_after(returned[ORDER[0]], here)
    return local_call(inverse_kernel, [(2, PLANES, GRID * GRID)], [work])(
        *returned, *own, *other, right_table(index, 1.0), left_table(index, mixed, 1.0)
    )[0]


def solution(mesh):
    return jax.shard_map(
        apply_exchange,
        mesh=mesh,
        in_specs=(P("band", "fft", None),),
        out_specs=P("band", "fft", None),
        check_vma=False,
    )
```

```python
import math

import jax
import jax.numpy as jnp
from jax import lax
from jax.experimental import pallas as pl
from jax.experimental.pallas import tpu as pltpu
from jax.sharding import PartitionSpec as P


GRID = 64
EXX_FRACTION = 0.25
SCREEN = 0.05
PLANES = 8
LANES = 128


ORDER = (2, 6, 4, 7, 5, 3, 1)
REACH = (5, 3, 6, 2, 7, 1)


def split_table(table, axis):
    high = lax.reduce_precision(table, 8, 7)
    return jnp.concatenate([high, high, table - high], axis).astype(jnp.bfloat16)


def wave(rows, columns, direction):
    angles = (rows[:, None] * columns[None, :] % GRID).astype(jnp.float32) * (2.0 * math.pi / GRID)
    return jnp.cos(angles), direction * jnp.sin(angles)


def left_table(rows, columns, direction):
    cosine, sine = wave(rows, columns, direction)
    top = jnp.concatenate([cosine, -sine], 1)
    bottom = jnp.concatenate([sine, cosine], 1)
    return split_table(jnp.concatenate([top, bottom], 0), 1)


def right_table(index, direction):
    cosine, sine = wave(index, index, direction)
    zero = jnp.zeros_like(cosine)
    table = jnp.concatenate(
        [
            jnp.concatenate([cosine, zero, sine, zero], 1),
            jnp.concatenate([zero, cosine, zero, sine], 1),
            jnp.concatenate([-sine, zero, cosine, zero], 1),
            jnp.concatenate([zero, -sine, zero, cosine], 1),
        ],
        0,
    )
    return split_table(table, 0)


def filter_table(index, here):
    signed = jnp.where(index < GRID // 2, index, index - GRID).astype(jnp.float32)
    wavenum = signed * (2.0 * math.pi / GRID)
    y_indices = here * PLANES + index[:PLANES]
    y_signed = jnp.where(y_indices < GRID // 2, y_indices, y_indices - GRID).astype(jnp.float32)
    y_wavenum = y_signed * (2.0 * math.pi / GRID)
    wide = jnp.concatenate([wavenum, wavenum])
    squares = wavenum[None, :, None] ** 2 + y_wavenum[:, None, None] ** 2 + wide[None, None, :] ** 2
    guarded = jnp.where(squares > 0, squares, 1.0)
    kernel = jnp.where(
        squares > 0, (1.0 - jnp.exp(-guarded / (4.0 * SCREEN * SCREEN))) / guarded, 0.0
    )
    return kernel * (-EXX_FRACTION / float(GRID) ** 3)


def parts(values):
    high = values.astype(jnp.bfloat16)
    low = (values - high.astype(jnp.float32)).astype(jnp.bfloat16)
    return high, low


def times_left(table, values):
    high, low = parts(values)
    stacked = jnp.concatenate([high, low, high], 0)
    return jnp.dot(table, stacked, preferred_element_type=jnp.float32)


def times_right(values, table):
    high, low = parts(values)
    stacked = jnp.concatenate([high, low, high], 1)
    return jnp.dot(stacked, table, preferred_element_type=jnp.float32)


def pair_sources(own_refs, other_refs, part, y_half, low_lanes):
    columns = slice(y_half * LANES, (y_half + 1) * LANES)
    own, other = own_refs[part][:, columns], other_refs[part][:, columns]
    even = jnp.where(low_lanes, own, pltpu.roll(other, GRID, 1))
    odd = jnp.where(low_lanes, pltpu.roll(own, GRID, 1), other)
    return even, odd


def forward_kernel(orb_ref, *refs):
    own_refs, other_refs, (right_ref, left_ref) = refs[:2], refs[2:4], refs[4:6]
    out_refs, (pair_ref, work_ref) = refs[6:14], refs[14:]
    low_lanes = lax.broadcasted_iota(jnp.int32, (PLANES, LANES), 1) < GRID
    for y_half in range(GRID // 2):
        for part in range(2):
            even, odd = pair_sources(own_refs, other_refs, part, y_half, low_lanes)
            for i in range(2):
                tile = orb_ref[i, :, y_half * LANES : (y_half + 1) * LANES]
                turned = pltpu.roll(tile, GRID, 1)
                base = y_half * 2 * PLANES
                lanes = slice(part * LANES, (part + 1) * LANES)
                pair_ref[i, base : base + PLANES, lanes] = (
                    jnp.where(low_lanes, tile, turned) * even
                )
                pair_ref[i, base + PLANES : base + 2 * PLANES, lanes] = (
                    jnp.where(low_lanes, turned, tile) * odd
                )
    for i in range(2):
        result = times_right(pair_ref[i], right_ref[...])
        work_ref[0] = result[:, :LANES]
        work_ref[1] = result[:, LANES:]
        for x in range(0, PLANES, 2):
            columns = []
            for plane in (x, x + 1):
                rows = [work_ref[part, pl.ds(plane, GRID, stride=PLANES), :] for part in range(2)]
                columns.append(jnp.concatenate(rows, 0))
            result = times_left(left_ref[...], jnp.concatenate(columns, 1))
            for k in range(2):
                for part in range(2):
                    for block in range(8):
                        top = part * GRID + block * PLANES
                        out_refs[block][i, x + k, part] = result[
                            top : top + PLANES, k * LANES : (k + 1) * LANES
                        ]


def middle_kernel(*refs):
    in_refs, (forth_ref, back_ref, filter_ref), out_refs = refs[:8], refs[8:11], refs[11:]
    for i in range(2):
        for ky in range(0, PLANES, 2):
            columns = []
            for y in (ky, ky + 1):
                rows = []
                for part in range(2):
                    for block in range(8):
                        start = i * 128 + part * 8 + y
                        rows.append(in_refs[block][pl.ds(start, PLANES, stride=16), :])
                columns.append(jnp.concatenate(rows, 0))
            spectrum = times_left(forth_ref[...], jnp.concatenate(columns, 1))
            scale = jnp.concatenate([filter_ref[ky], filter_ref[ky + 1]], 1)
            spectrum = spectrum * jnp.concatenate([scale, scale], 0)
            result = times_left(back_ref[...], spectrum)
            for k in range(2):
                for part in range(2):
                    for block in range(8):
                        start = i * 128 + part * 8 + ky + k
                        top = part * GRID + block * PLANES
                        out_refs[block][pl.ds(start, PLANES, stride=16), :] = result[
                            top : top + PLANES, k * LANES : (k + 1) * LANES
                        ]


def inverse_kernel(*refs):
    in_refs, own_refs, other_refs = refs[:8], refs[8:10], refs[10:12]
    right_ref, left_ref, out_ref, work_ref = refs[12:]
    low_lanes = lax.broadcasted_iota(jnp.int32, (PLANES, LANES), 1) < GRID
    for i in range(2):
        for x in range(0, PLANES, 2):
            columns = []
            for plane in (x, x + 1):
                rows = [ref[i, plane, part] for part in range(2) for ref in in_refs]
                columns.append(jnp.concatenate(rows, 0))
            result = times_left(left_ref[...], jnp.concatenate(columns, 1))
            for k in range(2):
                for part in range(2):
                    work_ref[part, pl.ds(x + k, GRID, stride=PLANES), :] = result[
                        part * GRID : (part + 1) * GRID, k * LANES : (k + 1) * LANES
                    ]
        potential = times_right(jnp.concatenate([work_ref[0], work_ref[1]], 1), right_ref[...])
        for y_half in range(GRID // 2):
            sums = [0.0, 0.0]
            for part in range(2):
                pair = pair_sources(own_refs, other_refs, part, y_half, low_lanes)
                for odd in range(2):
                    base = (y_half * 2 + odd) * PLANES
                    values = potential[base : base + PLANES, part * LANES : (part + 1) * LANES]
                    sums[odd] = sums[odd] + values * pair[odd]
            even, odd = (s + pltpu.roll(s, GRID, 1) for s in sums)
            out_ref[i, :, y_half * LANES : (y_half + 1) * LANES] = jnp.where(low_lanes, even, odd)


def local_call(kernel, shapes, scratch):
    return pl.pallas_call(
        kernel,
        out_shape=[jax.ShapeDtypeStruct(shape, jnp.float32) for shape in shapes],
        scratch_shapes=scratch,
        compiler_params=pltpu.CompilerParams(vmem_limit_bytes=24 << 20),
    )


def band_of(x_half, z, core):
    return x_half * 16 + z * 2 + core


def fetch_sources(orbitals, here):
    cores = (0, 1)
    band = lax.axis_index("band")
    x_half, z = band // 16, band // 2 % 8
    handed = lax.ppermute(
        orbitals[1], "band", [(band_of(0, 0, c), band_of(1, 0, c)) for c in cores]
    )
    root = jnp.where(x_half == 1, handed, orbitals[0])
    arrived = {
        step: lax.ppermute(
            root, "band", [(band_of(h, 0, c), band_of(h, step, c)) for h in cores for c in cores]
        )
        for step in REACH
    }
    arrived[4] = lax.ppermute(
        arrived[5], "band", [(band_of(h, 5, c), band_of(h, 4, c)) for h in cores for c in cores]
    )
    first = root
    for step, value in arrived.items():
        first = jnp.where(z == step, value, first)
    index, mixed, first = indices_after(first, here)
    tables = right_table(index, -1.0), left_table(mixed, index, -1.0)
    second = lax.ppermute(first, "band", [(b, b ^ 16) for b in range(32)])
    own = (first, second)
    other = tuple(lax.ppermute(a, "band", [(b, b ^ 1) for b in range(32)]) for a in own)
    return own, other, tables


def exchange(blocks):
    results = list(blocks)
    for d in ORDER:
        results[d] = lax.ppermute(blocks[d], "fft", [(p, p ^ d) for p in range(8)])
    return results


def indices_after(value, here):
    index, value = lax.optimization_barrier((jnp.arange(GRID, dtype=jnp.int32), value))
    mixed = (index // PLANES ^ here) * PLANES + index % PLANES
    return index, mixed, value


def apply_exchange(orbitals):
    here = lax.axis_index("fft")
    own, other, (right, left) = fetch_sources(orbitals, here)
    rows = PLANES * GRID
    work = pltpu.VMEM((2, rows, LANES), jnp.float32)
    block = (2, PLANES, 2, PLANES, LANES)
    flat = (2 * PLANES * 2 * PLANES, LANES)
    spectrum = local_call(
        forward_kernel,
        [block] * 8,
        [pltpu.VMEM((2, rows, 2 * LANES), jnp.float32), work],
    )(orbitals, *own, *other, right, left)
    spectrum = exchange(spectrum)
    index, mixed, spectrum[ORDER[0]] = indices_after(spectrum[ORDER[0]], here)
    spectrum = [a.reshape(flat) for a in spectrum]
    filtered = local_call(middle_kernel, [flat] * 8, [])(
        *spectrum,
        left_table(index, mixed, -1.0),
        left_table(mixed, index, 1.0),
        filter_table(index, here),
    )
    returned = exchange([a.reshape(block) for a in filtered])
    index, mixed, returned[ORDER[0]] = indices_after(returned[ORDER[0]], here)
    return local_call(inverse_kernel, [(2, PLANES, GRID * GRID)], [work])(
        *returned, *own, *other, right_table(index, 1.0), left_table(index, mixed, 1.0)
    )[0]


def solution(mesh):
    return jax.shard_map(
        apply_exchange,
        mesh=mesh,
        in_specs=(P("band", "fft", None),),
        out_specs=P("band", "fft", None),
        check_vma=False,
    )
```

```python
import math

import jax
import jax.numpy as jnp
from jax import lax
from jax.experimental import pallas as pl
from jax.experimental.pallas import tpu as pltpu
from jax.sharding import PartitionSpec as P


GRID = 64
EXX_FRACTION = 0.25
SCREEN = 0.05
PLANES = 8
LANES = 128


ORDER = (2, 6, 4, 7, 5, 3, 1)
REACH = (5, 3, 6, 2, 7, 1)


def split_table(table, axis):
    high = lax.reduce_precision(table, 8, 7)
    return jnp.concatenate([high, high, table - high], axis).astype(jnp.bfloat16)


def wave(rows, columns, direction):
    angles = (rows[:, None] * columns[None, :] % GRID).astype(jnp.float32) * (2.0 * math.pi / GRID)
    return jnp.cos(angles), direction * jnp.sin(angles)


def left_table(rows, columns, direction):
    cosine, sine = wave(rows, columns, direction)
    top = jnp.concatenate([cosine, -sine], 1)
    bottom = jnp.concatenate([sine, cosine], 1)
    return split_table(jnp.concatenate([top, bottom], 0), 1)


def right_table(index, direction):
    cosine, sine = wave(index, index, direction)
    zero = jnp.zeros_like(cosine)
    table = jnp.concatenate(
        [
            jnp.concatenate([cosine, zero, sine, zero], 1),
            jnp.concatenate([zero, cosine, zero, sine], 1),
            jnp.concatenate([-sine, zero, cosine, zero], 1),
            jnp.concatenate([zero, -sine, zero, cosine], 1),
        ],
        0,
    )
    return split_table(table, 0)


def filter_table(index, here):
    signed = jnp.where(index < GRID // 2, index, index - GRID).astype(jnp.float32)
    wavenum = signed * (2.0 * math.pi / GRID)
    y_indices = here * PLANES + index[:PLANES]
    y_signed = jnp.where(y_indices < GRID // 2, y_indices, y_indices - GRID).astype(jnp.float32)
    y_wavenum = y_signed * (2.0 * math.pi / GRID)
    wide = jnp.concatenate([wavenum, wavenum])
    squares = wavenum[None, :, None] ** 2 + y_wavenum[:, None, None] ** 2 + wide[None, None, :] ** 2
    guarded = jnp.where(squares > 0, squares, 1.0)
    kernel = jnp.where(
        squares > 0, (1.0 - jnp.exp(-guarded / (4.0 * SCREEN * SCREEN))) / guarded, 0.0
    )
    return kernel * (-EXX_FRACTION / float(GRID) ** 3)


def parts(values):
    high = values.astype(jnp.bfloat16)
    low = (values - high.astype(jnp.float32)).astype(jnp.bfloat16)
    return high, low


def times_left(table, values):
    high, low = parts(values)
    stacked = jnp.concatenate([high, low, high], 0)
    return jnp.dot(table, stacked, preferred_element_type=jnp.float32)


def times_right(values, table):
    high, low = parts(values)
    stacked = jnp.concatenate([high, low, high], 1)
    return jnp.dot(stacked, table, preferred_element_type=jnp.float32)


def both_rows(tile, low_lanes):
    turned = pltpu.roll(tile, GRID, 1)
    return jnp.where(low_lanes, tile, turned), jnp.where(low_lanes, turned, tile)


def join_rows(first, second, low_lanes):
    return (
        jnp.where(low_lanes, first, pltpu.roll(second, GRID, 1)),
        jnp.where(low_lanes, pltpu.roll(first, GRID, 1), second),
    )


def low_half():
    return lax.broadcasted_iota(jnp.int32, (PLANES, LANES), 1) < GRID


def forward_kernel(orb_ref, *refs):
    source_refs, (right_ref, left_ref) = refs[:2], refs[2:4]
    out_refs, (pair_ref, work_ref) = refs[-10:-2], refs[-2:]
    low_lanes = low_half()
    for y_half in range(GRID // 2):
        columns = slice(y_half * LANES, (y_half + 1) * LANES)
        tiles = join_rows(orb_ref[0, :, columns], orb_ref[1, :, columns], low_lanes)
        for part in range(2):
            sources = both_rows(source_refs[part][:, columns], low_lanes)
            for odd in range(2):
                base = (y_half * 2 + odd) * PLANES
                pair_ref[base : base + PLANES, part * LANES : (part + 1) * LANES] = (
                    tiles[odd] * sources[odd]
                )
    result = times_right(pair_ref[...], right_ref[...])
    work_ref[0] = result[:, :LANES]
    work_ref[1] = result[:, LANES:]
    for x in range(0, PLANES, 2):
        columns = []
        for plane in (x, x + 1):
            rows = [work_ref[part, pl.ds(plane, GRID, stride=PLANES), :] for part in range(2)]
            columns.append(jnp.concatenate(rows, 0))
        result = times_left(left_ref[...], jnp.concatenate(columns, 1))
        for k in range(2):
            for part in range(2):
                for block in range(8):
                    top = part * GRID + block * PLANES
                    out_refs[block][0, x + k, part] = result[
                        top : top + PLANES, k * LANES : (k + 1) * LANES
                    ]


def middle_kernel(*refs):
    in_refs, (forth_ref, back_ref, filter_ref), out_refs = refs[:8], refs[8:11], refs[11:]
    for i in range(2):
        for ky in range(0, PLANES, 2):
            columns = []
            for y in (ky, ky + 1):
                rows = []
                for part in range(2):
                    for block in range(8):
                        start = i * 128 + part * 8 + y
                        rows.append(in_refs[block][pl.ds(start, PLANES, stride=16), :])
                columns.append(jnp.concatenate(rows, 0))
            spectrum = times_left(forth_ref[...], jnp.concatenate(columns, 1))
            scale = jnp.concatenate([filter_ref[ky], filter_ref[ky + 1]], 1)
            spectrum = spectrum * jnp.concatenate([scale, scale], 0)
            result = times_left(back_ref[...], spectrum)
            for k in range(2):
                for part in range(2):
                    for block in range(8):
                        start = i * 128 + part * 8 + ky + k
                        top = part * GRID + block * PLANES
                        out_refs[block][pl.ds(start, PLANES, stride=16), :] = result[
                            top : top + PLANES, k * LANES : (k + 1) * LANES
                        ]


def inverse_kernel(*refs):
    in_refs, source_refs = refs[:8], (refs[8:10], refs[10:12])
    right_ref, left_ref, out_ref, work_ref, sum_ref = refs[12:]
    low_lanes = low_half()
    for pair in range(2):
        for x in range(0, PLANES, 2):
            columns = []
            for plane in (x, x + 1):
                rows = [ref[pair, plane, part] for part in range(2) for ref in in_refs]
                columns.append(jnp.concatenate(rows, 0))
            result = times_left(left_ref[...], jnp.concatenate(columns, 1))
            for k in range(2):
                for part in range(2):
                    work_ref[part, pl.ds(x + k, GRID, stride=PLANES), :] = result[
                        part * GRID : (part + 1) * GRID, k * LANES : (k + 1) * LANES
                    ]
        potential = times_right(jnp.concatenate([work_ref[0], work_ref[1]], 1), right_ref[...])
        for y_half in range(GRID // 2):
            columns = slice(y_half * LANES, (y_half + 1) * LANES)
            sources = [both_rows(ref[:, columns], low_lanes) for ref in source_refs[pair]]
            sums = []
            for odd in range(2):
                base = (y_half * 2 + odd) * PLANES
                rows = slice(base, base + PLANES)
                values = potential[rows, :LANES] * sources[0][odd]
                values = values + potential[rows, LANES:] * sources[1][odd]
                if pair == 0:
                    sum_ref[rows] = values
                else:
                    sums.append(sum_ref[rows] + values)
            if sums:
                out_ref[0, :, columns], out_ref[1, :, columns] = join_rows(*sums, low_lanes)


def local_call(kernel, shapes, scratch):
    return pl.pallas_call(
        kernel,
        out_shape=[jax.ShapeDtypeStruct(shape, jnp.float32) for shape in shapes],
        scratch_shapes=scratch,
        compiler_params=pltpu.CompilerParams(vmem_limit_bytes=24 << 20),
    )


def forward_call(pair, blocks, *operands):
    shape = jax.ShapeDtypeStruct((2, PLANES, 2, PLANES, LANES), jnp.float32)
    rows = PLANES * GRID
    whole = pl.BlockSpec(memory_space=pltpu.VMEM)
    return pl.pallas_call(
        forward_kernel,
        grid=(1,),
        in_specs=[whole] * len(operands) + [pl.BlockSpec(memory_space=pl.ANY)] * len(blocks),
        out_specs=[pl.BlockSpec((1, PLANES, 2, PLANES, LANES), lambda _: (pair, 0, 0, 0, 0))] * 8,
        out_shape=[shape] * 8,
        scratch_shapes=[
            pltpu.VMEM((rows, 2 * LANES), jnp.float32),
            pltpu.VMEM((2, rows, LANES), jnp.float32),
        ],
        input_output_aliases={len(operands) + k: k for k in range(len(blocks))},
        compiler_params=pltpu.CompilerParams(vmem_limit_bytes=24 << 20),
    )(*operands, *blocks)


def band_of(x_half, z, core):
    return x_half * 16 + z * 2 + core


def fetch_sources(orbitals, here):
    cores = (0, 1)
    band = lax.axis_index("band")
    x_half, z = band // 16, band // 2 % 8
    handed = lax.ppermute(
        orbitals[1], "band", [(band_of(0, 0, c), band_of(1, 0, c)) for c in cores]
    )
    root = jnp.where(x_half == 1, handed, orbitals[0])
    arrived = {
        step: lax.ppermute(
            root, "band", [(band_of(h, 0, c), band_of(h, step, c)) for h in cores for c in cores]
        )
        for step in REACH
    }
    arrived[4] = lax.ppermute(
        arrived[5], "band", [(band_of(h, 5, c), band_of(h, 4, c)) for h in cores for c in cores]
    )
    first = root
    for step, value in arrived.items():
        first = jnp.where(z == step, value, first)
    index, mixed, first = indices_after(first, here)
    tables = right_table(index, -1.0), left_table(mixed, index, -1.0)
    second = lax.ppermute(first, "band", [(b, b ^ 16) for b in range(32)])
    own = (first, second)
    other = tuple(lax.ppermute(a, "band", [(b, b ^ 1) for b in range(32)]) for a in own)
    return own, other, tables


def exchange(blocks):
    results = list(blocks)
    for d in ORDER:
        results[d] = lax.ppermute(blocks[d], "fft", [(p, p ^ d) for p in range(8)])
    return results


def indices_after(value, here):
    index, value = lax.optimization_barrier((jnp.arange(GRID, dtype=jnp.int32), value))
    mixed = (index // PLANES ^ here) * PLANES + index % PLANES
    return index, mixed, value


def apply_exchange(orbitals):
    here = lax.axis_index("fft")
    own, other, (right, left) = fetch_sources(orbitals, here)
    rows = PLANES * GRID
    work = pltpu.VMEM((2, rows, LANES), jnp.float32)
    block = (2, PLANES, 2, PLANES, LANES)
    flat = (2 * PLANES * 2 * PLANES, LANES)
    spectrum = forward_call(0, [], orbitals, *own, right, left)
    spectrum = forward_call(1, spectrum, orbitals, *other, right, left)
    spectrum = exchange(spectrum)
    index, mixed, spectrum[ORDER[0]] = indices_after(spectrum[ORDER[0]], here)
    spectrum = [a.reshape(flat) for a in spectrum]
    filtered = local_call(middle_kernel, [flat] * 8, [])(
        *spectrum,
        left_table(index, mixed, -1.0),
        left_table(mixed, index, 1.0),
        filter_table(index, here),
    )
    returned = exchange([a.reshape(block) for a in filtered])
    index, mixed, returned[ORDER[0]] = indices_after(returned[ORDER[0]], here)
    total = pltpu.VMEM((rows, LANES), jnp.float32)
    return local_call(inverse_kernel, [(2, PLANES, GRID * GRID)], [work, total])(
        *returned, *own, *other, right_table(index, 1.0), left_table(index, mixed, 1.0)
    )[0]


def solution(mesh):
    return jax.shard_map(
        apply_exchange,
        mesh=mesh,
        in_specs=(P("band", "fft", None),),
        out_specs=P("band", "fft", None),
        check_vma=False,
    )
```

```python
import math

import jax
import jax.numpy as jnp
from jax import lax
from jax.experimental import pallas as pl
from jax.experimental.pallas import tpu as pltpu
from jax.sharding import PartitionSpec as P


GRID = 64
EXX_FRACTION = 0.25
SCREEN = 0.05
PLANES = 8
LANES = 128


ORDER = (6, 2, 3, 5, 1, 7, 4)
REACH = (5, 3, 6, 2, 7, 1)


def split_table(table, axis):
    high = lax.reduce_precision(table, 8, 7)
    return jnp.concatenate([high, high, table - high], axis).astype(jnp.bfloat16)


def wave(rows, columns, direction):
    angles = (rows[:, None] * columns[None, :] % GRID).astype(jnp.float32) * (2.0 * math.pi / GRID)
    return jnp.cos(angles), direction * jnp.sin(angles)


def left_table(rows, columns, direction):
    cosine, sine = wave(rows, columns, direction)
    top = jnp.concatenate([cosine, -sine], 1)
    bottom = jnp.concatenate([sine, cosine], 1)
    return split_table(jnp.concatenate([top, bottom], 0), 1)


def right_table(index, direction):
    cosine, sine = wave(index, index, direction)
    zero = jnp.zeros_like(cosine)
    table = jnp.concatenate(
        [
            jnp.concatenate([cosine, zero, sine, zero], 1),
            jnp.concatenate([zero, cosine, zero, sine], 1),
            jnp.concatenate([-sine, zero, cosine, zero], 1),
            jnp.concatenate([zero, -sine, zero, cosine], 1),
        ],
        0,
    )
    return split_table(table, 0)


def filter_table(index, here):
    signed = jnp.where(index < GRID // 2, index, index - GRID).astype(jnp.float32)
    wavenum = signed * (2.0 * math.pi / GRID)
    y_indices = here * PLANES + index[:PLANES]
    y_signed = jnp.where(y_indices < GRID // 2, y_indices, y_indices - GRID).astype(jnp.float32)
    y_wavenum = y_signed * (2.0 * math.pi / GRID)
    wide = jnp.concatenate([wavenum, wavenum])
    squares = wavenum[None, :, None] ** 2 + y_wavenum[:, None, None] ** 2 + wide[None, None, :] ** 2
    guarded = jnp.where(squares > 0, squares, 1.0)
    kernel = jnp.where(
        squares > 0, (1.0 - jnp.exp(-guarded / (4.0 * SCREEN * SCREEN))) / guarded, 0.0
    )
    return kernel * (-EXX_FRACTION / float(GRID) ** 3)


def parts(values):
    high = values.astype(jnp.bfloat16)
    low = (values - high.astype(jnp.float32)).astype(jnp.bfloat16)
    return high, low


def times_left(table, values):
    high, low = parts(values)
    stacked = jnp.concatenate([high, low, high], 0)
    return jnp.dot(table, stacked, preferred_element_type=jnp.float32)


def times_right(values, table):
    high, low = parts(values)
    stacked = jnp.concatenate([high, low, high], 1)
    return jnp.dot(stacked, table, preferred_element_type=jnp.float32)


def both_rows(tile, low_lanes):
    turned = pltpu.roll(tile, GRID, 1)
    return jnp.where(low_lanes, tile, turned), jnp.where(low_lanes, turned, tile)


def join_rows(first, second, low_lanes):
    return (
        jnp.where(low_lanes, first, pltpu.roll(second, GRID, 1)),
        jnp.where(low_lanes, pltpu.roll(first, GRID, 1), second),
    )


def low_half():
    return lax.broadcasted_iota(jnp.int32, (PLANES, LANES), 1) < GRID


def forward_kernel(orb_ref, *refs):
    source_refs, (right_ref, left_ref) = refs[:2], refs[2:4]
    out_refs, (pair_ref, work_ref) = refs[-10:-2], refs[-2:]
    low_lanes = low_half()
    for y_half in range(GRID // 2):
        columns = slice(y_half * LANES, (y_half + 1) * LANES)
        tiles = join_rows(orb_ref[0, :, columns], orb_ref[1, :, columns], low_lanes)
        for part in range(2):
            sources = both_rows(source_refs[part][:, columns], low_lanes)
            for odd in range(2):
                base = (y_half * 2 + odd) * PLANES
                pair_ref[base : base + PLANES, part * LANES : (part + 1) * LANES] = (
                    tiles[odd] * sources[odd]
                )
    result = times_right(pair_ref[...], right_ref[...])
    work_ref[0] = result[:, :LANES]
    work_ref[1] = result[:, LANES:]
    for x in range(0, PLANES, 2):
        columns = []
        for plane in (x, x + 1):
            rows = [work_ref[part, pl.ds(plane, GRID, stride=PLANES), :] for part in range(2)]
            columns.append(jnp.concatenate(rows, 0))
        result = times_left(left_ref[...], jnp.concatenate(columns, 1))
        for k in range(2):
            for part in range(2):
                for block in range(8):
                    top = part * GRID + block * PLANES
                    out_refs[block][0, x + k, part] = result[
                        top : top + PLANES, k * LANES : (k + 1) * LANES
                    ]


def middle_kernel(*refs):
    in_refs, (forth_ref, back_ref, filter_ref), out_refs = refs[:8], refs[8:11], refs[11:]
    for i in range(2):
        for ky in range(0, PLANES, 2):
            columns = []
            for y in (ky, ky + 1):
                rows = []
                for part in range(2):
                    for block in range(8):
                        start = i * 128 + part * 8 + y
                        rows.append(in_refs[block][pl.ds(start, PLANES, stride=16), :])
                columns.append(jnp.concatenate(rows, 0))
            spectrum = times_left(forth_ref[...], jnp.concatenate(columns, 1))
            scale = jnp.concatenate([filter_ref[ky], filter_ref[ky + 1]], 1)
            spectrum = spectrum * jnp.concatenate([scale, scale], 0)
            result = times_left(back_ref[...], spectrum)
            for k in range(2):
                for part in range(2):
                    for block in range(8):
                        start = i * 128 + part * 8 + ky + k
                        top = part * GRID + block * PLANES
                        out_refs[block][pl.ds(start, PLANES, stride=16), :] = result[
                            top : top + PLANES, k * LANES : (k + 1) * LANES
                        ]


def inverse_kernel(*refs):
    in_refs, source_refs = refs[:8], (refs[8:10], refs[10:12])
    right_ref, left_ref, out_ref, work_ref, sum_ref = refs[12:]
    low_lanes = low_half()
    for pair in range(2):
        for x in range(0, PLANES, 2):
            columns = []
            for plane in (x, x + 1):
                rows = [ref[pair, plane, part] for part in range(2) for ref in in_refs]
                columns.append(jnp.concatenate(rows, 0))
            result = times_left(left_ref[...], jnp.concatenate(columns, 1))
            for k in range(2):
                for part in range(2):
                    work_ref[part, pl.ds(x + k, GRID, stride=PLANES), :] = result[
                        part * GRID : (part + 1) * GRID, k * LANES : (k + 1) * LANES
                    ]
        potential = times_right(jnp.concatenate([work_ref[0], work_ref[1]], 1), right_ref[...])
        for y_half in range(GRID // 2):
            columns = slice(y_half * LANES, (y_half + 1) * LANES)
            sources = [both_rows(ref[:, columns], low_lanes) for ref in source_refs[pair]]
            sums = []
            for odd in range(2):
                base = (y_half * 2 + odd) * PLANES
                rows = slice(base, base + PLANES)
                values = potential[rows, :LANES] * sources[0][odd]
                values = values + potential[rows, LANES:] * sources[1][odd]
                if pair == 0:
                    sum_ref[rows] = values
                else:
                    sums.append(sum_ref[rows] + values)
            if sums:
                out_ref[0, :, columns], out_ref[1, :, columns] = join_rows(*sums, low_lanes)


def local_call(kernel, shapes, scratch):
    return pl.pallas_call(
        kernel,
        out_shape=[jax.ShapeDtypeStruct(shape, jnp.float32) for shape in shapes],
        scratch_shapes=scratch,
        compiler_params=pltpu.CompilerParams(vmem_limit_bytes=24 << 20),
    )


def forward_call(pair, blocks, *operands):
    shape = jax.ShapeDtypeStruct((2, PLANES, 2, PLANES, LANES), jnp.float32)
    rows = PLANES * GRID
    whole = pl.BlockSpec(memory_space=pltpu.VMEM)
    return pl.pallas_call(
        forward_kernel,
        grid=(1,),
        in_specs=[whole] * len(operands) + [pl.BlockSpec(memory_space=pl.ANY)] * len(blocks),
        out_specs=[pl.BlockSpec((1, PLANES, 2, PLANES, LANES), lambda _: (pair, 0, 0, 0, 0))] * 8,
        out_shape=[shape] * 8,
        scratch_shapes=[
            pltpu.VMEM((rows, 2 * LANES), jnp.float32),
            pltpu.VMEM((2, rows, LANES), jnp.float32),
        ],
        input_output_aliases={len(operands) + k: k for k in range(len(blocks))},
        compiler_params=pltpu.CompilerParams(vmem_limit_bytes=24 << 20),
    )(*operands, *blocks)


def band_of(x_half, z, core):
    return x_half * 16 + z * 2 + core


def fetch_sources(orbitals, here):
    cores = (0, 1)
    band = lax.axis_index("band")
    x_half, z = band // 16, band // 2 % 8
    handed = lax.ppermute(
        orbitals[1], "band", [(band_of(0, 0, c), band_of(1, 0, c)) for c in cores]
    )
    root = jnp.where(x_half == 1, handed, orbitals[0])
    arrived = {
        step: lax.ppermute(
            root, "band", [(band_of(h, 0, c), band_of(h, step, c)) for h in cores for c in cores]
        )
        for step in REACH
    }
    arrived[4] = lax.ppermute(
        arrived[5], "band", [(band_of(h, 5, c), band_of(h, 4, c)) for h in cores for c in cores]
    )
    first = root
    for step, value in arrived.items():
        first = jnp.where(z == step, value, first)
    index, sent, _, first = indices_after(first, here)
    tables = right_table(index, -1.0), left_table(sent, index, -1.0)
    second = lax.ppermute(first, "band", [(b, b ^ 16) for b in range(32)])
    own = (first, second)
    other = tuple(lax.ppermute(a, "band", [(b, b ^ 1) for b in range(32)]) for a in own)
    return own, other, tables


def partner(p, block, sign):
    return (p // 4 ^ block // 4) * 4 + (p + sign * block) % 4


def exchange(blocks):
    results = list(blocks)
    for d in ORDER:
        pairs = [(p, partner(p, d, 1)) for p in range(8)]
        results[d] = lax.ppermute(blocks[d], "fft", pairs)
    return results


def indices_after(value, here):
    index, value = lax.optimization_barrier((jnp.arange(GRID, dtype=jnp.int32), value))
    sent, received = (
        partner(here, index // PLANES, sign) * PLANES + index % PLANES for sign in (1, -1)
    )
    return index, sent, received, value


def apply_exchange(orbitals):
    here = lax.axis_index("fft")
    own, other, (right, left) = fetch_sources(orbitals, here)
    rows = PLANES * GRID
    work = pltpu.VMEM((2, rows, LANES), jnp.float32)
    block = (2, PLANES, 2, PLANES, LANES)
    flat = (2 * PLANES * 2 * PLANES, LANES)
    spectrum = forward_call(0, [], orbitals, *own, right, left)
    spectrum = forward_call(1, spectrum, orbitals, *other, right, left)
    spectrum = exchange(spectrum)
    index, sent, received, spectrum[ORDER[0]] = indices_after(spectrum[ORDER[0]], here)
    spectrum = [a.reshape(flat) for a in spectrum]
    filtered = local_call(middle_kernel, [flat] * 8, [])(
        *spectrum,
        left_table(index, received, -1.0),
        left_table(sent, index, 1.0),
        filter_table(index, here),
    )
    returned = exchange([a.reshape(block) for a in filtered])
    index, _, received, returned[ORDER[0]] = indices_after(returned[ORDER[0]], here)
    total = pltpu.VMEM((rows, LANES), jnp.float32)
    return local_call(inverse_kernel, [(2, PLANES, GRID * GRID)], [work, total])(
        *returned, *own, *other, right_table(index, 1.0), left_table(index, received, 1.0)
    )[0]


def solution(mesh):
    return jax.shard_map(
        apply_exchange,
        mesh=mesh,
        in_specs=(P("band", "fft", None),),
        out_specs=P("band", "fft", None),
        check_vma=False,
    )
```
